32 devices in a mesh: lat: 8 (over y, x, core), lon: 4 (over z).
Axes of the slice: x: 2, y: 2, z: 4, core: 2. Of those that a mesh axis runs over, the one named last changes fastest.
Arguments:
- prediction_deviation: bfloat16 [16, 256, 128, 80], P(None, 'lat', 'lon'), may hold values from -6 to 6
- humid_energy_misfit: float32 [16, 256, 128], P(None, 'lat', 'lon'), may hold values from -0.6 to 0.6
- sensor_space_deviation: bfloat16 [8, 4, 80, 1024], P('lat', 'lon'), may hold values from -6 to 6
- scaled_departure: float32 [8, 4, 1024], P('lat', 'lon'), may hold values from -6 to 6
- datum_location: int32 [8, 4, 2, 1024], P('lat', 'lon'), may hold values from 0 to 31, as said below
- taper_category: int32 [8, 4, 1024], P('lat', 'lon'), may hold values from 0 to 3
- datum_patch_codes: int32 [8, 4, 4, 1024], P('lat', 'lon'), may hold values from -1 to 8, as said below
- active_datum_tally: int32 [8, 4], P('lat', 'lon'), may hold values from 128 to 1024, as said below
Outputs:
- impact: float32 [8, 4, 1024], P('lat', 'lon')
The draws below stay inside these ranges and needn't reach their ends.
Inputs may be any that keep to these rules, and one draw needn't show every extreme that they name: `datum_location`: row and column of the observation's cell, each from 0 to 31. `datum_patch_codes`: codes are 3 (dr + 1) + (ds + 1) for a tile offset (dr, ds) from the owner, or -1 for an empty entry. Entry 0 is always 4, the owner; the named codes of a slot are distinct and never name a tile beyond the first or last tile row. At least 128 live slots on every tile, and 1024 on some tile in every draw; slots from active_datum_tally on carry no observation.
All inputs are finite; a program needn't handle non-finite values.
Results may differ from the reference program's by a relative error of at most 0.0055.
Values may be sent and summed in bfloat16 or wider, within the bound.
A program may use at most 64 MiB of HBM per device.

```python
import jax
import jax.numpy as jnp
from jax import lax

RUN_TOTAL = 80
STRATA_TOTAL = 16
TW = 32
OBS_DEV = 1024
LAT_TILES = 8
LON_TILES = 4
NORTH_SOUTH_SPAN = 256
EAST_WEST_SPAN = 128


def obs_geometry(key):
    base = jax.random.fold_in(key, 7)
    first, second, third = jax.random.split(base, 3)
    array_shape = (LAT_TILES, LON_TILES, OBS_DEV)
    rows_drawn = jax.random.randint(first, array_shape, 0, TW, dtype=jnp.int32)
    cols_drawn = jax.random.randint(second, array_shape, 0, TW, dtype=jnp.int32)
    classes = jax.random.randint(third, array_shape, 0, 4, dtype=jnp.int32)
    return (rows_drawn, cols_drawn, classes)


def draw_humid_energy_misfit(key, part):
    base = jax.random.fold_in(key, 23)
    first = jax.random.fold_in(base, 0)
    array_shape = (STRATA_TOTAL, NORTH_SOUTH_SPAN, EAST_WEST_SPAN)
    drawn = 0.1 * jnp.clip(jax.random.normal(first, array_shape, jnp.float32), -6.0, 6.0)
    return drawn.astype(jnp.float32)


def draw_scaled_departure(key, part):
    base = jax.random.fold_in(key, 29)
    first = jax.random.fold_in(base, 0)
    array_shape = (LAT_TILES, LON_TILES, OBS_DEV)
    drawn = jnp.clip(jax.random.normal(first, array_shape, jnp.float32), -6.0, 6.0)
    return drawn.astype(jnp.float32)


def draw_datum_location(key, part):
    rows_drawn, cols_drawn, classes = obs_geometry(key)
    return jnp.stack([rows_drawn, cols_drawn], axis=2).astype(jnp.int32)


def draw_taper_category(key, part):
    rows_drawn, cols_drawn, classes = obs_geometry(key)
    return classes


def draw_datum_patch_codes(key, part):
    rows_drawn, cols_drawn, classes = obs_geometry(key)
    skipping = jax.random.randint(jax.random.fold_in(key, 13), rows_drawn.shape, 0, 8, dtype=jnp.int32)
    reach_cells = TW * (1 + classes)
    tile_rows = jnp.arange(LAT_TILES, dtype=jnp.int32)[:, None, None]
    upward = (8 * (rows_drawn + 1) < reach_cells) & (tile_rows > 0)
    downward = (8 * (TW - rows_drawn) < reach_cells) & (tile_rows < LAT_TILES - 1)
    leftward = 8 * (cols_drawn + 1) < reach_cells
    rightward = 8 * (TW - cols_drawn) < reach_cells
    row_step = jnp.where(upward, -1, jnp.where(downward, 1, 0))
    col_step = jnp.where(leftward, -1, jnp.where(rightward, 1, 0))
    has_row = upward | downward
    has_col = leftward | rightward
    own_code = jnp.full(rows_drawn.shape, 4, jnp.int32)
    row_code = jnp.where(has_row & (skipping != 1), 3 * (row_step + 1) + 1, -1)
    col_code = jnp.where(has_col & (skipping != 2), 3 + col_step + 1, -1)
    corner_code = jnp.where(has_row & has_col & (skipping != 0), 3 * (row_step + 1) + col_step + 1, -1)
    return jnp.stack([own_code, row_code, col_code, corner_code], axis=2).astype(jnp.int32)


def draw_active_datum_tally(key, part):
    base = jax.random.fold_in(key, 11)
    first, second, third, fourth = jax.random.split(base, 4)
    array_shape = (LAT_TILES, LON_TILES)
    drawn = jax.random.randint(first, array_shape, OBS_DEV // 8, OBS_DEV // 2 + 1, dtype=jnp.int32)
    crowded = jax.random.randint(second, array_shape, 0, 4, dtype=jnp.int32) == 0
    dense = OBS_DEV - jax.random.randint(third, array_shape, 0, OBS_DEV // 8, dtype=jnp.int32)
    counts = jnp.where(crowded, dense, drawn)
    chosen = jax.random.randint(fourth, (), 0, LAT_TILES * LON_TILES, dtype=jnp.int32)
    flat_index = jnp.arange(LAT_TILES * LON_TILES, dtype=jnp.int32).reshape(array_shape)
    return jnp.where(flat_index == chosen, OBS_DEV, counts).astype(jnp.int32)


def steps_of(key, extent, cuts, smallest, top_value):
    factor_of, own = 1.0, jax.random.fold_in(key, 6)
    for dim, shards_of in cuts:
        draws = jnp.exp(jax.random.uniform(jax.random.fold_in(own, dim), (shards_of,), jnp.float32, smallest / len(cuts), top_value / len(cuts)))
        factor_of = factor_of * jnp.repeat(draws, extent[dim] // shards_of).reshape([-1 if axis == dim else 1 for axis in range(len(extent))])
    return factor_of


def noise(own_key, dims, spread, bound, pieces=(), kind=jnp.bfloat16):
    factor_of = steps_of(own_key, dims, pieces, -0.22, 0.18) if pieces else 1.0
    array = jax.random.normal(own_key, dims, jnp.float32) * spread * factor_of
    return jnp.minimum(jnp.maximum(array, -bound), bound).astype(kind)


def setup_inputs(seed: int = 0) -> dict:
    key_list = jax.random.split(jax.random.key(seed), 9)
    prediction_deviation = noise(key_list[0], (STRATA_TOTAL, NORTH_SOUTH_SPAN, EAST_WEST_SPAN, RUN_TOTAL), 1.0, 6.0, ((1, 8), (2, 4)))
    humid_energy_misfit = draw_humid_energy_misfit(jax.random.fold_in(key_list[8], 71), 0)
    sensor_space_deviation = noise(key_list[2], (LAT_TILES, LON_TILES, RUN_TOTAL, OBS_DEV), 1.0, 6.0, ((0, 8), (1, 4)))
    scaled_departure = draw_scaled_departure(jax.random.fold_in(key_list[8], 71), 0)
    datum_location = draw_datum_location(jax.random.fold_in(key_list[8], 71), 0)
    taper_category = draw_taper_category(jax.random.fold_in(key_list[8], 71), 0)
    datum_patch_codes = draw_datum_patch_codes(jax.random.fold_in(key_list[8], 71), 0)
    active_datum_tally = draw_active_datum_tally(jax.random.fold_in(key_list[8], 71), 0)
    return dict(prediction_deviation=prediction_deviation, humid_energy_misfit=humid_energy_misfit, sensor_space_deviation=sensor_space_deviation, scaled_departure=scaled_departure, datum_location=datum_location, taper_category=taper_category, datum_patch_codes=datum_patch_codes, active_datum_tally=active_datum_tally)


def taper_weights(obs_row, obs_col, obs_class, cell_rows, cell_cols, allowed, patch_span_points):
    radius = patch_span_points * (1.0 + obs_class) * 0.125
    radius_sq = (radius * radius)[:, None]
    distance = (cell_rows[None, :] - obs_row[:, None]) ** 2 + (cell_cols[None, :] - obs_col[:, None]) ** 2
    fraction = 1.0 - distance / radius_sq
    return jnp.where(allowed & (distance < radius_sq), fraction * fraction, 0.0).astype(jnp.bfloat16)


def tile_offset(shifted, patch_span_points):
    return (shifted >= patch_span_points).astype(jnp.int32) - (shifted < 0).astype(jnp.int32)


def reference(prediction_deviation, humid_energy_misfit, sensor_space_deviation, scaled_departure, datum_location, taper_category, datum_patch_codes, active_datum_tally):
    patch_span_points = TW
    margin = TW // 2
    window_width = 2 * TW

    def add_level(stratum_index, summed):
        altitude_stratum = lax.dynamic_index_in_dim(prediction_deviation, stratum_index, 0, keepdims=False).astype(jnp.float32)
        weight = lax.dynamic_index_in_dim(humid_energy_misfit, stratum_index, 0, keepdims=False)
        return summed + altitude_stratum * weight[..., None]

    summed = lax.fori_loop(0, STRATA_TOTAL, add_level, jnp.zeros((NORTH_SOUTH_SPAN, EAST_WEST_SPAN, RUN_TOTAL), jnp.float32))
    projected = summed.astype(jnp.bfloat16)
    padded = jnp.pad(projected, ((margin, margin), (0, 0), (0, 0)))
    padded = jnp.concatenate([padded[:, EAST_WEST_SPAN - margin:], padded, padded[:, :margin]], axis=1)

    offsets = jnp.arange(window_width, dtype=jnp.int32) - margin
    rel_rows = jnp.repeat(offsets, window_width)
    rel_cols = jnp.tile(offsets, window_width)
    tile_code = 3 * (tile_offset(rel_rows, patch_span_points) + 1) + tile_offset(rel_cols, patch_span_points) + 1
    cell_rows = rel_rows.astype(jnp.float32)
    cell_cols = rel_cols.astype(jnp.float32)

    tile_total = LAT_TILES * LON_TILES
    anomaly_all = sensor_space_deviation.reshape(tile_total, RUN_TOTAL, OBS_DEV)
    innovation_all = scaled_departure.reshape(tile_total, OBS_DEV)
    place_all = datum_location.reshape(tile_total, 2, OBS_DEV)
    class_all = taper_category.reshape(tile_total, OBS_DEV)
    cover_all = datum_patch_codes.reshape(tile_total, 4, OBS_DEV)
    count_all = active_datum_tally.reshape(tile_total)

    def one_tile(tile_index):
        tile_row = tile_index // LON_TILES
        tile_col = tile_index % LON_TILES
        window = lax.dynamic_slice(padded, (tile_row * patch_span_points, tile_col * patch_span_points, jnp.int32(0)),
                                   (window_width, window_width, RUN_TOTAL)).reshape(window_width * window_width, RUN_TOTAL)
        anomaly = lax.dynamic_index_in_dim(anomaly_all, tile_index, 0, keepdims=False)
        scaled = lax.dynamic_index_in_dim(innovation_all, tile_index, 0, keepdims=False)
        position = lax.dynamic_index_in_dim(place_all, tile_index, 0, keepdims=False).astype(jnp.float32)
        taper_size = lax.dynamic_index_in_dim(class_all, tile_index, 0, keepdims=False).astype(jnp.float32)
        cover_codes = lax.dynamic_index_in_dim(cover_all, tile_index, 0, keepdims=False)
        count_here = lax.dynamic_index_in_dim(count_all, tile_index, 0, keepdims=False)
        allowed = jnp.any(cover_codes[:, :, None] == tile_code[None, None, :], axis=0)
        weights = taper_weights(position[0], position[1], taper_size, cell_rows, cell_cols, allowed, patch_span_points)
        projection = jnp.dot(weights.astype(jnp.float32), window.astype(jnp.float32),
                             precision=lax.Precision.HIGHEST)
        summed_here = jnp.sum(projection * anomaly.T.astype(jnp.float32), axis=1)
        live_slots = (jnp.arange(OBS_DEV, dtype=jnp.int32) < count_here).astype(jnp.float32)
        return scaled * summed_here / (RUN_TOTAL - 1) * live_slots

    impacts = lax.map(one_tile, jnp.arange(tile_total, dtype=jnp.int32))
    return impacts.reshape(LAT_TILES, LON_TILES, OBS_DEV)
```

```python
import functools

import jax
import jax.numpy as jnp
from jax import lax
from jax.experimental import pallas as pl
from jax.experimental.pallas import tpu as pltpu
from jax.sharding import PartitionSpec as P

MESH = pl.DeviceIdType.MESH
READ_CHUNKS = 4


def kernel(
    nlat, nlon,
    dev_hbm, mis_hbm, sens_hbm, scaled_hbm, loc_hbm, cat_hbm, codes_hbm, tally_hbm,
    out_ref,
    dev, mis, sens, scaled, loc, cat, codes, tally,
    split, cells, own, halo, bound, taper, acc,
    in_sem, dev_sem, send_sem, recv_sem,
):
    levels, tile, _, members = dev.shape
    half = tile // 2
    slots = sens.shape[1]
    p = lax.axis_index("lat")
    q = lax.axis_index("lon")
    left = lax.rem(q + nlon - 1, nlon)
    right = lax.rem(q + 1, nlon)
    has_up = p > 0
    has_down = p < nlat - 1

    rows_per = tile // READ_CHUNKS
    small = [
        pltpu.make_async_copy(src, dst, in_sem.at[i])
        for i, (src, dst) in enumerate(
            [(mis_hbm, mis), (loc_hbm, loc), (cat_hbm, cat), (codes_hbm, codes),
             (sens_hbm, sens), (scaled_hbm, scaled), (tally_hbm, tally)]
        )
    ]
    reads = [
        pltpu.make_async_copy(
            dev_hbm.at[:, pl.ds(c * rows_per, rows_per)],
            dev.at[:, pl.ds(c * rows_per, rows_per)],
            dev_sem.at[c],
        )
        for c in range(READ_CHUNKS)
    ]
    small[0].start()
    reads[0].start()
    for copy in small[1:4]:
        copy.start()
    for copy in reads[1:]:
        copy.start()
    for copy in small[4:]:
        copy.start()

    barrier = pltpu.get_barrier_semaphore()

    def greet(row):
        for col in (left, q, right):
            pl.semaphore_signal(barrier, inc=1, device_id=(row, col), device_id_type=MESH)

    for col in (left, right):
        pl.semaphore_signal(barrier, inc=1, device_id=(p, col), device_id_type=MESH)
    pl.when(has_up)(lambda: greet(p - 1))
    pl.when(has_down)(lambda: greet(p + 1))

    small[0].wait()
    wide = jnp.concatenate([mis[l] for l in range(levels)], axis=1)
    high = wide.astype(jnp.bfloat16).astype(jnp.float32)
    split[0] = high
    split[1] = wide - high

    for copy in small[1:4]:
        copy.wait()
    place = loc[...].astype(jnp.float32)
    radius = (tile * 0.125) * (1.0 + cat[...].astype(jnp.float32))
    radius_sq = radius * radius
    cover = codes[...]
    barred = [
        jnp.where(jnp.any(cover == code, axis=0, keepdims=True), 0.0, 4.0 * half * half)
        for code in range(9)
    ]
    for j in range(4):
        b = lax.broadcasted_iota(jnp.int32, (half, slots), 0).astype(jnp.float32) + (j - 1) * half
        gap = b - place[1:2]
        gap = gap * gap
        ds = (j + 1) // 2
        for dr in range(3):
            bound[dr * 4 + j] = (gap + barred[3 * dr + ds]).astype(jnp.bfloat16)

    diagonal = (
        lax.rem(lax.broadcasted_iota(jnp.int32, (tile, levels * tile), 1), tile)
        == lax.broadcasted_iota(jnp.int32, (tile, levels * tile), 0)
    )

    peers = 2 + 3 * jnp.minimum(p, 1) + 3 * jnp.minimum(nlat - 1 - p, 1)
    pl.semaphore_wait(barrier, peers)

    def send(yh, xh, kind):
        i = 3 if yh == 0 else 0
        j = 3 if xh == 0 else 0
        row = p - 1 if yh == 0 else p + 1
        col = left if xh == 0 else right
        if kind == "row":
            i, row = yh + 1, p
        if kind == "col":
            j, col = xh + 1, q
        slot = i * 4 + j
        copy = pltpu.make_async_remote_copy(
            src_ref=own.at[2 * yh + xh],
            dst_ref=halo.at[slot],
            send_sem=send_sem.at[slot],
            recv_sem=recv_sem.at[slot],
            device_id=(row, col),
            device_id_type=MESH,
        )
        return slot, copy, kind != "row"

    copies = {}
    for yh in range(2):
        for c in range(yh * READ_CHUNKS // 2, (yh + 1) * READ_CHUNKS // 2):
            reads[c].wait()

        def level_sum(y, _):
            row = yh * half + y
            terms = []
            for s in range(2):
                line = split[s, pl.ds(row, 1), :]
                terms.append(
                    jnp.where(diagonal, jnp.broadcast_to(line, diagonal.shape), 0.0).astype(jnp.bfloat16)
                )
            both = jnp.dot(
                jnp.concatenate(terms, axis=0),
                dev[:, row].reshape(levels * tile, members),
                preferred_element_type=jnp.float32,
            )
            total = both[:tile] + both[tile:]
            cells[0, y] = total[:half]
            cells[1, y] = total[half:]
            return 0

        lax.fori_loop(0, half, level_sum, 0, unroll=4)
        for xh in range(2):
            own[2 * yh + xh] = cells[xh].reshape(half * half, members).T.astype(jnp.bfloat16)
            for kind in ("row", "corner", "col"):
                slot, copy, vertical = send(yh, xh, kind)
                copies[slot] = copy
                if vertical:
                    pl.when(has_up if yh == 0 else has_down)(copy.start)
                else:
                    copy.start()

    row_gap = jnp.broadcast_to(place[0:1], (half, slots)).astype(jnp.bfloat16)
    reach = jnp.broadcast_to(radius_sq, (half, slots)).astype(jnp.bfloat16)
    for i in (1, 2, 0, 3):
        dr = (i + 1) // 2

        def build(y, gap):
            room = reach - gap * gap
            for j in range(4):
                t = jnp.maximum(room - bound[dr * 4 + j], jnp.bfloat16(0))
                taper[i * 4 + j, y] = t * t
            return gap - jnp.bfloat16(1)

        lax.fori_loop(0, half, build, row_gap - jnp.bfloat16((i - 1) * half), unroll=2)

    def product(slot, source):
        return jnp.dot(
            source,
            taper[slot].reshape(half * half, slots),
            preferred_element_type=jnp.float32,
        )

    def add(slot, copy):
        copy.wait_recv()
        acc[...] += product(slot, halo[slot])

    for yh in range(2):
        for xh in range(2):
            value = product((yh + 1) * 4 + xh + 1, own[2 * yh + xh])
            if yh == 0 and xh == 0:
                acc[...] = value
            else:
                acc[...] += value
    for slot in (1, 2, 13, 14, 4, 7, 8, 11, 0, 3, 12, 15):
        if slot < 4:
            pl.when(has_up)(functools.partial(add, slot, copies[slot]))
        elif slot >= 12:
            pl.when(has_down)(functools.partial(add, slot, copies[slot]))
        else:
            add(slot, copies[slot])

    for copy in small[4:]:
        copy.wait()
    summed = jnp.sum(acc[...] * sens[...].astype(jnp.float32), axis=0, keepdims=True)
    live = lax.broadcasted_iota(jnp.int32, (1, slots), 1) < jnp.broadcast_to(tally[...], (1, slots))
    value = scaled[...] * summed / ((members - 1) * radius_sq * radius_sq)
    out_ref[...] = jnp.where(live, value, 0.0)

    for slot, copy in copies.items():
        if slot < 4:
            pl.when(has_down)(copy.wait_send)
        elif slot >= 12:
            pl.when(has_up)(copy.wait_send)
        else:
            copy.wait_send()


def on_device(nlat, nlon, dev, mis, sens, scaled, loc, cat, codes, tally):
    levels, tile, _, members = dev.shape
    slots = sens.shape[3]
    half = tile // 2
    quad = half * half
    bf16, f32, i32 = jnp.bfloat16, jnp.float32, jnp.int32
    out = pl.pallas_call(
        functools.partial(kernel, nlat, nlon),
        out_shape=jax.ShapeDtypeStruct((1, slots), f32),
        in_specs=[pl.BlockSpec(memory_space=pl.ANY)] * 8,
        out_specs=pl.BlockSpec(memory_space=pltpu.VMEM),
        scratch_shapes=[
            pltpu.VMEM((levels, tile, tile, members), bf16),
            pltpu.VMEM((levels, tile, tile), f32),
            pltpu.VMEM((members, slots), bf16),
            pltpu.VMEM((1, slots), f32),
            pltpu.VMEM((2, slots), i32),
            pltpu.VMEM((1, slots), i32),
            pltpu.VMEM((4, slots), i32),
            pltpu.VMEM((1, 1), i32),
            pltpu.VMEM((2, tile, levels * tile), f32),
            pltpu.VMEM((2, half, half, members), f32),
            pltpu.VMEM((4, members, quad), bf16),
            pltpu.VMEM((16, members, quad), bf16),
            pltpu.VMEM((12, half, slots), bf16),
            pltpu.VMEM((16, half, half, slots), bf16),
            pltpu.VMEM((members, slots), f32),
            pltpu.SemaphoreType.DMA((7,)),
            pltpu.SemaphoreType.DMA((READ_CHUNKS,)),
            pltpu.SemaphoreType.DMA((16,)),
            pltpu.SemaphoreType.DMA((16,)),
        ],
        compiler_params=pltpu.CompilerParams(
            collective_id=0, has_side_effects=True, vmem_limit_bytes=60 * 1024 * 1024
        ),
    )(dev, mis, sens[0, 0], scaled[0], loc[0, 0], cat[0], codes[0, 0], tally)
    return out[None]


def solution(mesh):
    return jax.shard_map(
        functools.partial(on_device, mesh.shape["lat"], mesh.shape["lon"]),
        mesh=mesh,
        in_specs=(
            P(None, "lat", "lon", None),
            P(None, "lat", "lon"),
            P("lat", "lon", None, None),
            P("lat", "lon", None),
            P("lat", "lon", None, None),
            P("lat", "lon", None),
            P("lat", "lon", None, None),
            P("lat", "lon"),
        ),
        out_specs=P("lat", "lon", None),
        check_vma=False,
    )
```

```python
import functools

import jax
import jax.numpy as jnp
from jax import lax
from jax.experimental import pallas as pl
from jax.experimental.pallas import tpu as pltpu
from jax.sharding import PartitionSpec as P

MESH = pl.DeviceIdType.MESH
HALF_CHUNKS = 2


def kernel(
    nlat, nlon,
    dev_hbm, mis_hbm, sens_hbm, scaled_hbm, loc_hbm, cat_hbm, codes_hbm, tally_hbm,
    out_ref,
    dev, mis, sens, scaled, loc, cat, codes, tally,
    split, cells, own, halo, bound, taper, acc,
    in_sem, dev_sem, send_sem, recv_sem,
):
    levels, tile, _, members = dev.shape
    half = tile // 2
    slots = sens.shape[1]
    p = lax.axis_index("lat")
    q = lax.axis_index("lon")
    left = lax.rem(q + nlon - 1, nlon)
    right = lax.rem(q + 1, nlon)
    has_up = p > 0
    has_down = p < nlat - 1

    first = 1 - lax.rem(p, 2)
    halves = (first, 1 - first)
    has_first = jnp.where(first == 1, nlat - 1 - p, p) > 0
    has_second = jnp.where(first == 1, p, nlat - 1 - p) > 0
    rows_per = half // HALF_CHUNKS
    small = [
        pltpu.make_async_copy(src, dst, in_sem.at[i])
        for i, (src, dst) in enumerate(
            [(mis_hbm, mis), (loc_hbm, loc), (cat_hbm, cat), (codes_hbm, codes),
             (sens_hbm, sens), (scaled_hbm, scaled), (tally_hbm, tally)]
        )
    ]
    reads = []
    for yh in halves:
        for c in range(HALF_CHUNKS):
            rows = pl.ds(yh * half + c * rows_per, rows_per)
            reads.append(
                pltpu.make_async_copy(dev_hbm.at[:, rows], dev.at[:, rows], dev_sem.at[len(reads)])
            )
    small[0].start()
    reads[0].start()
    for copy in small[1:4]:
        copy.start()
    for copy in reads[1:]:
        copy.start()
    for copy in small[4:]:
        copy.start()

    barrier = pltpu.get_barrier_semaphore()

    def greet(row):
        for col in (left, q, right):
            pl.semaphore_signal(barrier, inc=1, device_id=(row, col), device_id_type=MESH)

    for col in (left, right):
        pl.semaphore_signal(barrier, inc=1, device_id=(p, col), device_id_type=MESH)
    pl.when(has_up)(lambda: greet(p - 1))
    pl.when(has_down)(lambda: greet(p + 1))

    small[0].wait()
    wide = jnp.concatenate([mis[l] for l in range(levels)], axis=1)
    high = wide.astype(jnp.bfloat16).astype(jnp.float32)
    split[0] = high
    split[1] = wide - high

    for copy in small[1:4]:
        copy.wait()
    place = loc[...].astype(jnp.float32)
    radius = (tile * 0.125) * (1.0 + cat[...].astype(jnp.float32))
    radius_sq = radius * radius
    cover = codes[...]
    barred = [
        jnp.where(jnp.any(cover == code, axis=0, keepdims=True), 0.0, 4.0 * half * half)
        for code in range(9)
    ]
    for j in range(4):
        b = lax.broadcasted_iota(jnp.int32, (half, slots), 0).astype(jnp.float32) + (j - 1) * half
        gap = b - place[1:2]
        gap = gap * gap
        ds = (j + 1) // 2
        for dr in range(3):
            bound[dr * 4 + j] = (gap + barred[3 * dr + ds]).astype(jnp.bfloat16)

    diagonal = (
        lax.rem(lax.broadcasted_iota(jnp.int32, (tile, levels * tile), 1), tile)
        == lax.broadcasted_iota(jnp.int32, (tile, levels * tile), 0)
    )

    peers = 2 + 3 * jnp.minimum(p, 1) + 3 * jnp.minimum(nlat - 1 - p, 1)
    pl.semaphore_wait(barrier, peers)

    def remote(src, slot, row, col):
        return pltpu.make_async_remote_copy(
            src_ref=src,
            dst_ref=halo.at[slot],
            send_sem=send_sem.at[slot],
            recv_sem=recv_sem.at[slot],
            device_id=(row, col),
            device_id_type=MESH,
        )

    for stage, yh in enumerate(halves):
        def level_sum(y, _):
            row = yh * half + y
            terms = []
            for s in range(2):
                line = split[s, pl.ds(row, 1), :]
                terms.append(
                    jnp.where(diagonal, jnp.broadcast_to(line, diagonal.shape), 0.0).astype(jnp.bfloat16)
                )
            both = jnp.dot(
                jnp.concatenate(terms, axis=0),
                dev[:, row].reshape(levels * tile, members),
                preferred_element_type=jnp.float32,
            )
            total = both[:tile] + both[tile:]
            cells[0, y] = total[:half]
            cells[1, y] = total[half:]
            return 0

        for c in range(HALF_CHUNKS):
            reads[stage * HALF_CHUNKS + c].wait()
            lax.fori_loop(c * rows_per, (c + 1) * rows_per, level_sum, 0, unroll=True)
        beyond = p + 2 * yh - 1
        edge = 12 * (1 - yh)
        for xh in range(2):
            j, col = (3, left) if xh == 0 else (0, right)
            mine = 2 * yh + xh
            own[mine] = cells[xh].reshape(half * half, members).T.astype(jnp.bfloat16)
            source = own.at[mine]
            remote(source, 4 * (yh + 1) + j, p, col).start()
            if stage == 0:
                pl.when(has_first)(remote(source, edge + xh + 1, beyond, q).start)
            else:
                @pl.when(has_second)
                def _():
                    remote(source, edge + j, beyond, col).start()
                    remote(source, edge + xh + 1, beyond, q).start()

    def relay(j):
        slot = 4 * (first + 1) + j
        remote(halo.at[slot], slot, p, right).wait_recv()
        copy = remote(halo.at[slot], 12 * (1 - first) + j, p + 2 * first - 1, q)
        pl.when(has_first)(copy.start)

    near = 3 * (1 - jnp.minimum(q, 1))
    copies = {
        slot: remote(own.at[0], slot, p, right)
        for slot in (1, 2, 13, 14, 4, 7, 8, 11, 0, 3, 12, 15)
    }

    row_gap = jnp.broadcast_to(place[0:1], (half, slots)).astype(jnp.bfloat16)
    reach = jnp.broadcast_to(radius_sq, (half, slots)).astype(jnp.bfloat16)
    for i in (1, 2, 0, 3):
        dr = (i + 1) // 2

        def build(y, gap):
            room = reach - gap * gap
            for j in range(4):
                t = jnp.maximum(room - bound[dr * 4 + j], jnp.bfloat16(0))
                taper[i * 4 + j, y] = t * t
            return gap - jnp.bfloat16(1)

        lax.fori_loop(0, half, build, row_gap - jnp.bfloat16((i - 1) * half), unroll=2)

    def product(slot, source):
        return jnp.dot(
            source,
            taper[slot].reshape(half * half, slots),
            preferred_element_type=jnp.float32,
        )

    def add(slot):
        acc[...] += product(slot, halo[slot])

    def receive(slot):
        copies[slot].wait_recv()
        add(slot)

    relay(near)
    for yh in range(2):
        for xh in range(2):
            value = product((yh + 1) * 4 + xh + 1, own[2 * yh + xh])
            if yh == 0 and xh == 0:
                acc[...] = value
            else:
                acc[...] += value
    for slot in (1, 2, 13, 14):
        pl.when(has_up if slot < 4 else has_down)(functools.partial(receive, slot))
    relay(3 - near)
    for yh in range(2):
        for slot in (4 * yh + 4, 4 * yh + 7):
            pl.when(first != yh)(copies[slot].wait_recv)
            add(slot)
    for slot in (0, 3, 12, 15):
        pl.when(has_up if slot < 4 else has_down)(functools.partial(receive, slot))

    for copy in small[4:]:
        copy.wait()
    summed = jnp.sum(acc[...] * sens[...].astype(jnp.float32), axis=0, keepdims=True)
    live = lax.broadcasted_iota(jnp.int32, (1, slots), 1) < jnp.broadcast_to(tally[...], (1, slots))
    value = scaled[...] * summed / ((members - 1) * radius_sq * radius_sq)
    out_ref[...] = jnp.where(live, value, 0.0)

    for slot, copy in copies.items():
        if slot < 4:
            pl.when(has_down)(copy.wait_send)
        elif slot >= 12:
            pl.when(has_up)(copy.wait_send)
        else:
            copy.wait_send()


def on_device(nlat, nlon, dev, mis, sens, scaled, loc, cat, codes, tally):
    levels, tile, _, members = dev.shape
    slots = sens.shape[3]
    half = tile // 2
    quad = half * half
    bf16, f32, i32 = jnp.bfloat16, jnp.float32, jnp.int32
    out = pl.pallas_call(
        functools.partial(kernel, nlat, nlon),
        out_shape=jax.ShapeDtypeStruct((1, slots), f32),
        in_specs=[pl.BlockSpec(memory_space=pl.ANY)] * 8,
        out_specs=pl.BlockSpec(memory_space=pltpu.VMEM),
        scratch_shapes=[
            pltpu.VMEM((levels, tile, tile, members), bf16),
            pltpu.VMEM((levels, tile, tile), f32),
            pltpu.VMEM((members, slots), bf16),
            pltpu.VMEM((1, slots), f32),
            pltpu.VMEM((2, slots), i32),
            pltpu.VMEM((1, slots), i32),
            pltpu.VMEM((4, slots), i32),
            pltpu.VMEM((1, 1), i32),
            pltpu.VMEM((2, tile, levels * tile), f32),
            pltpu.VMEM((2, half, half, members), f32),
            pltpu.VMEM((4, members, quad), bf16),
            pltpu.VMEM((16, members, quad), bf16),
            pltpu.VMEM((12, half, slots), bf16),
            pltpu.VMEM((16, half, half, slots), bf16),
            pltpu.VMEM((members, slots), f32),
            pltpu.SemaphoreType.DMA((7,)),
            pltpu.SemaphoreType.DMA((2 * HALF_CHUNKS,)),
            pltpu.SemaphoreType.DMA((16,)),
            pltpu.SemaphoreType.DMA((16,)),
        ],
        compiler_params=pltpu.CompilerParams(
            collective_id=0, has_side_effects=True, vmem_limit_bytes=60 * 1024 * 1024
        ),
    )(dev, mis, sens[0, 0], scaled[0], loc[0, 0], cat[0], codes[0, 0], tally)
    return out[None]


def solution(mesh):
    return jax.shard_map(
        functools.partial(on_device, mesh.shape["lat"], mesh.shape["lon"]),
        mesh=mesh,
        in_specs=(
            P(None, "lat", "lon", None),
            P(None, "lat", "lon"),
            P("lat", "lon", None, None),
            P("lat", "lon", None),
            P("lat", "lon", None, None),
            P("lat", "lon", None),
            P("lat", "lon", None, None),
            P("lat", "lon"),
        ),
        out_specs=P("lat", "lon", None),
        check_vma=False,
    )
```

```python
import functools

import jax
import jax.numpy as jnp
from jax import lax
from jax.experimental import pallas as pl
from jax.experimental.pallas import tpu as pltpu
from jax.sharding import PartitionSpec as P

MESH = pl.DeviceIdType.MESH
HALF_CHUNKS = 2


def kernel(
    nlat, nlon,
    dev_hbm, mis_hbm, sens_hbm, scaled_hbm, loc_hbm, cat_hbm, codes_hbm, tally_hbm,
    out_ref,
    dev, mis, sens, scaled, loc, cat, codes, tally,
    split, cells, own, halo, bound, taper, acc,
    in_sem, dev_sem, send_sem, recv_sem,
):
    levels, tile, _, members = dev.shape
    half = tile // 2
    slots = sens.shape[1]
    p = lax.axis_index("lat")
    q = lax.axis_index("lon")
    left = lax.rem(q + nlon - 1, nlon)
    right = lax.rem(q + 1, nlon)
    has_up = p > 0
    has_down = p < nlat - 1

    first = lax.rem(p, 2)
    halves = (first, 1 - first)
    present = [jnp.where(yh == 1, nlat - 1 - p, p) > 0 for yh in halves]
    rows_per = half // HALF_CHUNKS
    small = [
        pltpu.make_async_copy(src, dst, in_sem.at[i])
        for i, (src, dst) in enumerate(
            [(mis_hbm, mis), (loc_hbm, loc), (cat_hbm, cat), (codes_hbm, codes),
             (sens_hbm, sens), (scaled_hbm, scaled), (tally_hbm, tally)]
        )
    ]
    reads = []
    for yh in halves:
        for c in range(HALF_CHUNKS):
            rows = pl.ds(yh * half + c * rows_per, rows_per)
            reads.append(
                pltpu.make_async_copy(dev_hbm.at[:, rows], dev.at[:, rows], dev_sem.at[len(reads)])
            )
    small[0].start()
    reads[0].start()
    for copy in small[1:4]:
        copy.start()
    for copy in reads[1:]:
        copy.start()
    for copy in small[4:]:
        copy.start()

    barrier = pltpu.get_barrier_semaphore()

    def greet(row):
        for col in (left, q, right):
            pl.semaphore_signal(barrier, inc=1, device_id=(row, col), device_id_type=MESH)

    for col in (left, right):
        pl.semaphore_signal(barrier, inc=1, device_id=(p, col), device_id_type=MESH)
    pl.when(has_up)(lambda: greet(p - 1))
    pl.when(has_down)(lambda: greet(p + 1))

    small[0].wait()
    wide = jnp.concatenate([mis[l] for l in range(levels)], axis=1)
    high = wide.astype(jnp.bfloat16).astype(jnp.float32)
    split[0] = high
    split[1] = wide - high

    for copy in small[1:4]:
        copy.wait()
    place = loc[...].astype(jnp.float32)
    radius = (tile * 0.125) * (1.0 + cat[...].astype(jnp.float32))
    radius_sq = radius * radius
    cover = codes[...]
    barred = [
        jnp.where(jnp.any(cover == code, axis=0, keepdims=True), 0.0, 4.0 * half * half)
        for code in range(9)
    ]
    for j in range(4):
        b = lax.broadcasted_iota(jnp.int32, (half, slots), 0).astype(jnp.float32) + (j - 1) * half
        gap = b - place[1:2]
        gap = gap * gap
        ds = (j + 1) // 2
        for dr in range(3):
            bound[dr * 4 + j] = (gap + barred[3 * dr + ds]).astype(jnp.bfloat16)

    diagonal = (
        lax.rem(lax.broadcasted_iota(jnp.int32, (tile, levels * tile), 1), tile)
        == lax.broadcasted_iota(jnp.int32, (tile, levels * tile), 0)
    )

    def remote(src, slot, row, col):
        return pltpu.make_async_remote_copy(
            src_ref=src,
            dst_ref=halo.at[slot],
            send_sem=send_sem.at[slot],
            recv_sem=recv_sem.at[slot],
            device_id=(row, col),
            device_id_type=MESH,
        )

    for stage, yh in enumerate(halves):
        def level_sum(y, _):
            row = yh * half + y
            terms = []
            for s in range(2):
                line = split[s, pl.ds(row, 1), :]
                terms.append(
                    jnp.where(diagonal, jnp.broadcast_to(line, diagonal.shape), 0.0).astype(jnp.bfloat16)
                )
            both = jnp.dot(
                jnp.concatenate(terms, axis=0),
                dev[:, row].reshape(levels * tile, members),
                preferred_element_type=jnp.float32,
            )
            total = both[:tile] + both[tile:]
            cells[0, y] = total[:half]
            cells[1, y] = total[half:]
            return 0

        for c in range(HALF_CHUNKS):
            reads[stage * HALF_CHUNKS + c].wait()
            lax.fori_loop(c * rows_per, (c + 1) * rows_per, level_sum, 0, unroll=True)
        for xh in range(2):
            own[2 * yh + xh] = cells[xh].reshape(half * half, members).T.astype(jnp.bfloat16)
        if stage == 0:
            peers = 2 + 3 * jnp.minimum(p, 1) + 3 * jnp.minimum(nlat - 1 - p, 1)
            pl.semaphore_wait(barrier, peers)
        beyond = p + 2 * yh - 1
        edge = 12 * (1 - yh)
        for xh in range(2):
            j, col = (3, left) if xh == 0 else (0, right)
            mine = 2 * yh + xh
            source = own.at[mine]
            remote(source, 4 * (yh + 1) + j, p, col).start()
            pl.when(present[stage])(remote(source, edge + xh + 1, beyond, q).start)

    def relay(stage, j):
        yh = halves[stage]
        slot = 4 * (yh + 1) + j
        remote(halo.at[slot], slot, p, right).wait_recv()
        copy = remote(halo.at[slot], 12 * (1 - yh) + j, p + 2 * yh - 1, q)
        pl.when(present[stage])(copy.start)

    near = 3 * (1 - jnp.minimum(q, 1))
    copies = {
        slot: remote(own.at[0], slot, p, right)
        for slot in (1, 2, 13, 14, 4, 7, 8, 11, 0, 3, 12, 15)
    }

    row_gap = jnp.broadcast_to(place[0:1], (half, slots)).astype(jnp.bfloat16)
    reach = jnp.broadcast_to(radius_sq, (half, slots)).astype(jnp.bfloat16)
    for i in (1, 2, 0, 3):
        dr = (i + 1) // 2

        def build(y, gap):
            room = reach - gap * gap
            for j in range(4):
                t = jnp.maximum(room - bound[dr * 4 + j], jnp.bfloat16(0))
                taper[i * 4 + j, y] = t * t
            return gap - jnp.bfloat16(1)

        lax.fori_loop(0, half, build, row_gap - jnp.bfloat16((i - 1) * half), unroll=2)

    def product(slot, source):
        return jnp.dot(
            source,
            taper[slot].reshape(half * half, slots),
            preferred_element_type=jnp.float32,
        )

    def add(slot):
        acc[...] += product(slot, halo[slot])

    def receive(slot):
        copies[slot].wait_recv()
        add(slot)

    relay(0, near)
    for yh in range(2):
        for xh in range(2):
            value = product((yh + 1) * 4 + xh + 1, own[2 * yh + xh])
            if yh == 0 and xh == 0:
                acc[...] = value
            else:
                acc[...] += value
    for slot in (1, 2, 13, 14):
        pl.when(has_up if slot < 4 else has_down)(functools.partial(receive, slot))
    relay(1, near)
    relay(0, 3 - near)
    relay(1, 3 - near)
    for yh in range(2):
        for slot in (4 * yh + 4, 4 * yh + 7):
            add(slot)
    for slot in (0, 3, 12, 15):
        pl.when(has_up if slot < 4 else has_down)(functools.partial(receive, slot))

    for copy in small[4:]:
        copy.wait()
    summed = jnp.sum(acc[...] * sens[...].astype(jnp.float32), axis=0, keepdims=True)
    live = lax.broadcasted_iota(jnp.int32, (1, slots), 1) < jnp.broadcast_to(tally[...], (1, slots))
    value = scaled[...] * summed / ((members - 1) * radius_sq * radius_sq)
    out_ref[...] = jnp.where(live, value, 0.0)

    for slot, copy in copies.items():
        if slot < 4:
            pl.when(has_down)(copy.wait_send)
        elif slot >= 12:
            pl.when(has_up)(copy.wait_send)
        else:
            copy.wait_send()


def on_device(nlat, nlon, dev, mis, sens, scaled, loc, cat, codes, tally):
    levels, tile, _, members = dev.shape
    slots = sens.shape[3]
    half = tile // 2
    quad = half * half
    bf16, f32, i32 = jnp.bfloat16, jnp.float32, jnp.int32
    out = pl.pallas_call(
        functools.partial(kernel, nlat, nlon),
        out_shape=jax.ShapeDtypeStruct((1, slots), f32),
        in_specs=[pl.BlockSpec(memory_space=pl.ANY)] * 8,
        out_specs=pl.BlockSpec(memory_space=pltpu.VMEM),
        scratch_shapes=[
            pltpu.VMEM((levels, tile, tile, members), bf16),
            pltpu.VMEM((levels, tile, tile), f32),
            pltpu.VMEM((members, slots), bf16),
            pltpu.VMEM((1, slots), f32),
            pltpu.VMEM((2, slots), i32),
            pltpu.VMEM((1, slots), i32),
            pltpu.VMEM((4, slots), i32),
            pltpu.VMEM((1, 1), i32),
            pltpu.VMEM((2, tile, levels * tile), f32),
            pltpu.VMEM((2, half, half, members), f32),
            pltpu.VMEM((4, members, quad), bf16),
            pltpu.VMEM((16, members, quad), bf16),
            pltpu.VMEM((12, half, slots), bf16),
            pltpu.VMEM((16, half, half, slots), bf16),
            pltpu.VMEM((members, slots), f32),
            pltpu.SemaphoreType.DMA((7,)),
            pltpu.SemaphoreType.DMA((2 * HALF_CHUNKS,)),
            pltpu.SemaphoreType.DMA((16,)),
            pltpu.SemaphoreType.DMA((16,)),
        ],
        compiler_params=pltpu.CompilerParams(
            collective_id=0, has_side_effects=True, vmem_limit_bytes=60 * 1024 * 1024
        ),
    )(dev, mis, sens[0, 0], scaled[0], loc[0, 0], cat[0], codes[0, 0], tally)
    return out[None]


def solution(mesh):
    return jax.shard_map(
        functools.partial(on_device, mesh.shape["lat"], mesh.shape["lon"]),
        mesh=mesh,
        in_specs=(
            P(None, "lat", "lon", None),
            P(None, "lat", "lon"),
            P("lat", "lon", None, None),
            P("lat", "lon", None),
            P("lat", "lon", None, None),
            P("lat", "lon", None),
            P("lat", "lon", None, None),
            P("lat", "lon"),
        ),
        out_specs=P("lat", "lon", None),
        check_vma=False,
    )
```
